32 devices in a mesh: row: 4 (over z), col: 8 (over y, x, core).
Axes of the slice: x: 2, y: 2, z: 4, core: 2. Of those that a mesh axis runs over, the one named last changes fastest.
Arguments:
- positions: float32 [3, 65536], P(None, ('row', 'col')), may hold values from 0 to 1
- masses: float32 [1, 65536], P(None, ('row', 'col')), may hold values from 2e-09 to 2e-08
- counts: int32 [1, 512], P(None, ('row', 'col')), may hold values from 32 to 128
- sources: int32 [512, 8], P(('row', 'col')), may hold values from 0 to 47, as said below
Outputs:
- accel: float32 [3, 65536], P(None, ('row', 'col'))
The draws below stay inside these ranges and needn't reach their ends.
Inputs may be any that keep to these rules, and one draw needn't show every extreme that they name: `sources`: each device's source ids name exactly 4 distinct leaves of the lower row neighbour and exactly 4 of the upper one.
All inputs are finite; a program needn't handle non-finite values.
Results may differ from the reference program's by a relative error of at most 0.00024.
Values sent between devices are 32-bit elements; how exact they have to be, the bound alone decides.
A program may use at most 64 MiB of HBM per device.

```python
import math
import jax
import jax.numpy as jnp
from jax import lax

LEAF = 128
K = 8
BLK = 2
NL = 16
REQ = 4
ROWS = 65536
N_ROW = 4
N_COL = 8
DEVICES = 32


cell_width = 0.0025


def draw_sources(key, part):

    def one_device(device):
        sub = jax.random.fold_in(jax.random.fold_in(key, 7011), device)
        key_low, key_high, key_rest, key_perm = jax.random.split(sub, 4)
        low_pick = jax.random.permutation(key_low, NL)[:REQ].astype(jnp.int32) + NL
        high_pick = jax.random.permutation(key_high, NL)[:REQ].astype(jnp.int32) + 2 * NL
        candidates = jnp.concatenate([jnp.arange(NL, dtype=jnp.int32), low_pick, high_pick])
        chosen = jax.random.randint(key_rest, (NL * K - 2 * REQ,), 0, NL + 2 * REQ)
        listed = jnp.concatenate([low_pick, high_pick, candidates[chosen]])
        order = jax.random.permutation(key_perm, NL * K)
        return listed[order].reshape(NL, K)
    return jax.vmap(one_device)(jnp.arange(DEVICES, dtype=jnp.int32)).reshape(DEVICES * NL, K)


def draw_positions(key, part):
    sub = jax.random.fold_in(key, 5123)
    key_leaf, key_slot = jax.random.split(sub, 2)
    index = jnp.arange(ROWS, dtype=jnp.int32)
    per_device = NL * LEAF
    sender = index // per_device
    row_index = (sender // N_COL).astype(jnp.float32)
    target_col = (index % per_device // (BLK * LEAF)).astype(jnp.float32)
    leaf_index = index // LEAF
    radius = N_ROW * cell_width / (2.0 * jnp.pi)
    angle = 2.0 * jnp.pi * row_index / N_ROW
    centre_x = 0.5 + radius * jnp.cos(angle)
    centre_y = 0.5 + radius * jnp.sin(angle)
    centre_z = 0.5 + (target_col - N_COL / 2.0) * 3.0 * cell_width
    centres = jnp.stack([centre_x, centre_y, centre_z])
    leaf_jitter = jax.random.uniform(key_leaf, (3, ROWS // LEAF), jnp.float32, -0.5, 0.5) * cell_width
    slot_offset = jax.random.uniform(key_slot, (3, ROWS), jnp.float32, -0.5, 0.5) * cell_width
    return (centres + leaf_jitter[:, leaf_index] + slot_offset).astype(jnp.float32)


def place_ends(values, rng, low, top_value):
    longest = values.shape.index(max(values.shape))
    spots = []
    for shift in (0, 1):
        where = [jax.random.randint(jax.random.fold_in(rng, axis), (), 0, length) for axis, length in enumerate(values.shape)]
        where[longest] = (where[longest] + shift) % values.shape[longest]
        spots.append(tuple(where))
    return values.at[spots[0]].set(low).at[spots[1]].set(top_value)


def shard_levels(stream_key, shape, cuts, least, high):
    factor_of, own = 1.0, jax.random.fold_in(stream_key, 6)
    for axis_at, blocks in cuts:
        steps = jnp.exp(jax.random.uniform(jax.random.fold_in(own, axis_at), (blocks,), jnp.float32, least / len(cuts), high / len(cuts)))
        factor_of = factor_of * jnp.repeat(steps, shape[axis_at] // blocks).reshape([-1 if axis == axis_at else 1 for axis in range(len(shape))])
    return factor_of


def setup_inputs(seed: int = 0) -> dict:
    streams_of = jax.random.split(jax.random.key(seed), 5)
    positions = draw_positions(jax.random.fold_in(streams_of[4], 71), 0)
    masses = jnp.clip(jnp.exp(math.log(1.999999987845058e-08) - 2.3025851 * jax.random.uniform(streams_of[1], (1, ROWS), jnp.float32) ** shard_levels(streams_of[1], (1, ROWS), ((1, 32),), -0.2, 0.2)), 1.999999943436137e-09, 1.999999987845058e-08)
    counts = place_ends(jax.random.randint(streams_of[2], (1, DEVICES * NL), LEAF // 4, LEAF + 1), jax.random.fold_in(streams_of[2], 1), LEAF // 4, LEAF).astype(jnp.int32)
    sources = draw_sources(jax.random.fold_in(streams_of[4], 71), 0)
    return {"positions": positions, "masses": masses, "counts": counts, "sources": sources}


softening = 2.5e-07

def leaf_forces(full_table, targets, sources, alive):
    count = targets.shape[0]
    width = targets.shape[2]
    target_groups = targets.reshape(count // 8, 8, 4, width)
    source_groups = sources.reshape(count // 8, 8, sources.shape[1])
    alive_groups = alive.reshape(count // 8, 8, width)

    def one_group(items):
        target, index, living = items
        source = full_table[index]
        delta_x = source[:, :, 0, None, :] - target[:, None, 0, :, None]
        delta_y = source[:, :, 1, None, :] - target[:, None, 1, :, None]
        delta_z = source[:, :, 2, None, :] - target[:, None, 2, :, None]
        spread = softening + delta_x * delta_x + delta_y * delta_y + delta_z * delta_z
        weight = source[:, :, 3, None, :] / (spread * jnp.sqrt(spread))
        pull_x = lax.optimization_barrier(jnp.sum(weight * delta_x, axis=(1, 3)))
        pull_y = lax.optimization_barrier(jnp.sum(weight * delta_y, axis=(1, 3)))
        pull_z = lax.optimization_barrier(jnp.sum(weight * delta_z, axis=(1, 3)))
        return jnp.stack([pull_x, pull_y, pull_z], axis=1) * living[:, None, :]
    out = lax.map(one_group, (target_groups, source_groups, alive_groups))
    return out.reshape(count, 3, width)

def reference(positions, masses, counts, sources):
    rows_n, cols_n = (N_ROW, N_COL)
    coords = positions.reshape(3, rows_n, cols_n, cols_n, BLK, LEAF).transpose(1, 3, 2, 4, 0, 5).reshape(rows_n, cols_n, NL, 3, LEAF)
    weights = masses.reshape(1, rows_n, cols_n, cols_n, BLK, LEAF).transpose(1, 3, 2, 4, 0, 5).reshape(rows_n, cols_n, NL, 1, LEAF)
    livecount = counts.reshape(rows_n, cols_n, cols_n, BLK).transpose(0, 2, 1, 3).reshape(rows_n, cols_n, NL)
    alive = (jnp.arange(LEAF, dtype=jnp.int32)[None, None, None, :] < livecount[..., None]).astype(jnp.float32)
    table = jnp.concatenate([coords, weights * alive[:, :, :, None, :]], axis=3)
    full = jnp.concatenate([table, jnp.roll(table, 1, axis=0), jnp.roll(table, -1, axis=0)], axis=2)
    full = full.reshape(rows_n * cols_n, 3 * NL, 4, LEAF)
    lists = sources.reshape(rows_n * cols_n, NL, K)
    alive_all = alive.reshape(rows_n * cols_n, NL, LEAF)

    def device_forces(items):
        whole, index, living = items
        return leaf_forces(whole, whole[:NL], index, living)
    result = lax.map(device_forces, (full, lists, alive_all))
    return result.transpose(2, 0, 1, 3).reshape(3, ROWS)
```

```python
import functools

import jax
import jax.numpy as jnp
from jax import lax
from jax.experimental import pallas as pl
from jax.experimental.pallas import tpu as pltpu
from jax.sharding import PartitionSpec as P

softening = 2.5e-07
COMPONENTS = 4
CHUNK = 32
GROUP = 16
MESH = pl.DeviceIdType.MESH


def exchange_kernel(
    rows, cols, pos_hbm, mass_hbm, counts_hbm, table,
    pos, mass, counts, packed, in_sems, own_sem, send, recv, up_send, down_send, low_recv, high_recv,
):
    r, c = lax.axis_index("row"), lax.axis_index("col")
    up, down = lax.rem(r + 1, rows), lax.rem(r + rows - 1, rows)
    loads = [
        pltpu.make_async_copy(src, dst, in_sems.at[i])
        for i, (src, dst) in enumerate(((pos_hbm, pos), (mass_hbm, mass), (counts_hbm, counts)))
    ]
    for load in loads:
        load.start()

    barrier = pltpu.get_barrier_semaphore()
    pl.semaphore_signal(barrier, inc=1, device_id=(up, c), device_id_type=MESH)
    pl.semaphore_signal(barrier, inc=1, device_id=(down, c), device_id_type=MESH)

    def greet(o, carry):
        peer = lax.rem(c + o, cols)
        pl.semaphore_signal(barrier, inc=1, device_id=(r, peer), device_id_type=MESH)
        return carry

    lax.fori_loop(1, cols, greet, 0)
    for load in loads:
        load.wait()

    tile = packed.shape[1]
    blk = tile // COMPONENTS
    width = packed.shape[2]
    lane = lax.broadcasted_iota(jnp.int32, (1, width), 1)

    def pack(p, carry):
        for b in range(blk):
            leaf = p * blk + b
            here = pl.ds(pl.multiple_of(leaf * width, width), width)
            packed[p, COMPONENTS * b : COMPONENTS * b + 3, :] = pos[:, here]
            packed[p, COMPONENTS * b + 3 : COMPONENTS * b + 4, :] = jnp.where(
                lane < counts[0, leaf], mass[:, here], 0.0
            )
        return carry

    lax.fori_loop(0, cols, pack, 0, unroll=cols <= 8)
    pl.semaphore_wait(barrier, cols + 1)

    def across(o):
        peer = lax.rem(c + o, cols)
        return pltpu.make_async_remote_copy(
            src_ref=packed.at[peer], dst_ref=table.at[0, c],
            send_sem=send.at[peer], recv_sem=recv.at[c],
            device_id=(r, peer), device_id_type=MESH,
        )

    def along(src, p, to_up):
        return pltpu.make_async_remote_copy(
            src_ref=src, dst_ref=table.at[1 if to_up else 2, p],
            send_sem=(up_send if to_up else down_send).at[p],
            recv_sem=(low_recv if to_up else high_recv).at[p],
            device_id=(up if to_up else down, c), device_id_type=MESH,
        )

    def send_across(o, carry):
        across(o).start()
        return carry

    lax.fori_loop(1, cols, send_across, 0)
    along(packed.at[c], c, True).start()
    along(packed.at[c], c, False).start()
    own = pltpu.make_async_copy(packed.at[c], table.at[0, c], own_sem)
    own.start()

    def forward(o, carry):
        p = lax.bitwise_xor(c, o) if cols & (cols - 1) == 0 else lax.rem(c + o, cols)
        pltpu.make_async_remote_copy(
            src_ref=packed.at[p], dst_ref=table.at[0, p],
            send_sem=send.at[p], recv_sem=recv.at[p],
            device_id=(r, p), device_id_type=MESH,
        ).wait_recv()
        along(table.at[0, p], p, True).start()
        along(table.at[0, p], p, False).start()
        return carry

    lax.fori_loop(1, cols, forward, 0)
    own.wait()

    def settle_sends(o, carry):
        across(o).wait_send()
        return carry

    lax.fori_loop(1, cols, settle_sends, 0)

    def settle(p, carry):
        for to_up in (True, False):
            copy = along(table.at[0, p], p, to_up)
            copy.wait_send()
            copy.wait_recv()
        return carry

    lax.fori_loop(0, cols, settle, 0)


def exchange(rows, cols, positions, masses, counts):
    leaves = counts.shape[1]
    width = positions.shape[1] // leaves
    tile = COMPONENTS * (leaves // cols)
    dma = pltpu.SemaphoreType.DMA
    return pl.pallas_call(
        functools.partial(exchange_kernel, rows, cols),
        out_shape=jax.ShapeDtypeStruct((3, cols, tile, width), jnp.float32),
        in_specs=[pl.BlockSpec(memory_space=pl.ANY)] * 3,
        out_specs=pl.BlockSpec(memory_space=pltpu.VMEM),
        scratch_shapes=[
            pltpu.VMEM(positions.shape, jnp.float32),
            pltpu.VMEM(masses.shape, jnp.float32),
            pltpu.SMEM(counts.shape, jnp.int32),
            pltpu.VMEM((cols, tile, width), jnp.float32),
            dma((3,)), dma(()), dma((cols,)), dma((cols,)),
            dma((cols,)), dma((cols,)), dma((cols,)), dma((cols,)),
        ],
        compiler_params=pltpu.CompilerParams(collective_id=0, has_side_effects=True),
        name="exchange",
    )(positions, masses, counts)


def force_kernel(sources, table, out, spread_targets, pulls, live):
    width = table.shape[1]
    group = spread_targets.shape[0]
    per_list = sources.shape[1]
    ones = jnp.ones((8, width), jnp.float32)

    def one_group(g, carry):
        def prepare(i, carry):
            row = (g * group + i) * COMPONENTS
            for axis in range(3):
                line = table[pl.ds(row + axis, 1), :]
                spread_targets[i, axis] = jnp.broadcast_to(line, (width, width)).T
            alive = table[pl.ds(row + 3, 1), :] > 0.0
            live[i] = jnp.sum(alive.astype(jnp.int32))
            return carry

        lax.fori_loop(0, group, prepare, 0, unroll=4)

        def one_target(i, carry):
            ids = [sources[g * group + i, k] * COMPONENTS for k in range(per_list)]

            def one_chunk(n, carry):
                here = pl.ds(pl.multiple_of(n * CHUNK, CHUNK), CHUNK)
                tx, ty, tz = (spread_targets[i, axis, here, :] for axis in range(3))
                ax = ay = az = jnp.zeros((CHUNK, width), jnp.float32)
                for k in range(per_list):
                    dx = table[pl.ds(ids[k], 1), :] - tx
                    dy = table[pl.ds(ids[k] + 1, 1), :] - ty
                    dz = table[pl.ds(ids[k] + 2, 1), :] - tz
                    inverse = lax.rsqrt(softening + dx * dx + dy * dy + dz * dz)
                    weight = table[pl.ds(ids[k] + 3, 1), :] * inverse * (inverse * inverse)
                    ax, ay, az = ax + weight * dx, ay + weight * dy, az + weight * dz
                pulls[i, 0, here, :] = ax
                pulls[i, 1, here, :] = ay
                pulls[i, 2, here, :] = az
                return carry

            chunks = lax.div(live[i] + (CHUNK - 1), CHUNK)
            return lax.fori_loop(0, chunks, one_chunk, carry)

        lax.fori_loop(0, group, one_target, 0)

        def reduce(i, carry):
            t = g * group + i
            alive = table[pl.ds(t * COMPONENTS + 3, 1), :] > 0.0
            for axis in range(3):
                total = lax.dot_general(
                    ones, pulls[i, axis], (((1,), (1,)), ((), ())),
                    precision=lax.Precision.HIGHEST, preferred_element_type=jnp.float32,
                )
                out[axis : axis + 1, pl.ds(pl.multiple_of(t * width, width), width)] = jnp.where(
                    alive, total[0:1], 0.0
                )
            return carry

        lax.fori_loop(0, group, reduce, 0, unroll=4)
        return carry

    lax.fori_loop(0, sources.shape[0] // group, one_group, 0)


def forces(table, sources):
    leaves, width = sources.shape[0], table.shape[1]
    group = GROUP if leaves % GROUP == 0 else leaves
    return pl.pallas_call(
        force_kernel,
        out_shape=jax.ShapeDtypeStruct((3, leaves * width), jnp.float32),
        in_specs=[pl.BlockSpec(memory_space=pltpu.SMEM), pl.BlockSpec(memory_space=pltpu.VMEM)],
        out_specs=pl.BlockSpec(memory_space=pltpu.VMEM),
        scratch_shapes=[
            pltpu.VMEM((group, 3, width, width), jnp.float32),
            pltpu.VMEM((group, 3, width, width), jnp.float32),
            pltpu.SMEM((group,), jnp.int32),
        ],
        name="forces",
    )(sources, table)


def solution(mesh):
    rows, cols = mesh.shape["row"], mesh.shape["col"]

    def on_device(positions, masses, counts, sources):
        table = exchange(rows, cols, positions, masses, counts)
        return forces(table.reshape(-1, table.shape[-1]), sources)

    return jax.shard_map(
        on_device,
        mesh=mesh,
        in_specs=(
            P(None, ("row", "col")),
            P(None, ("row", "col")),
            P(None, ("row", "col")),
            P(("row", "col"), None),
        ),
        out_specs=P(None, ("row", "col")),
        check_vma=False,
    )
```

```python
import functools

import jax
import jax.numpy as jnp
from jax import lax
from jax.experimental import pallas as pl
from jax.experimental.pallas import tpu as pltpu
from jax.sharding import PartitionSpec as P

softening = 2.5e-07
COMPONENTS = 4
CHUNK = 32
GROUP = 16
VMEM_LIMIT = 16 * 2**20
MESH = pl.DeviceIdType.MESH


def exchange_kernel(
    rows, cols, pos_hbm, mass_hbm, counts_hbm, table,
    pos, mass, counts, packed, in_sems, own_sem, send, recv, up_send, down_send, low_recv, high_recv,
):
    r, c = lax.axis_index("row"), lax.axis_index("col")
    up, down = lax.rem(r + 1, rows), lax.rem(r + rows - 1, rows)
    loads = [
        pltpu.make_async_copy(src, dst, in_sems.at[i])
        for i, (src, dst) in enumerate(((pos_hbm, pos), (mass_hbm, mass), (counts_hbm, counts)))
    ]
    for load in loads:
        load.start()

    barrier = pltpu.get_barrier_semaphore()
    pl.semaphore_signal(barrier, inc=1, device_id=(up, c), device_id_type=MESH)
    pl.semaphore_signal(barrier, inc=1, device_id=(down, c), device_id_type=MESH)

    def greet(o, carry):
        peer = lax.rem(c + o, cols)
        pl.semaphore_signal(barrier, inc=1, device_id=(r, peer), device_id_type=MESH)
        return carry

    lax.fori_loop(1, cols, greet, 0)
    for load in loads:
        load.wait()

    tile = packed.shape[1]
    blk = tile // COMPONENTS
    width = packed.shape[2]
    lane = lax.broadcasted_iota(jnp.int32, (1, width), 1)

    def pack(p, carry):
        for b in range(blk):
            leaf = p * blk + b
            here = pl.ds(pl.multiple_of(leaf * width, width), width)
            packed[p, COMPONENTS * b : COMPONENTS * b + 3, :] = pos[:, here]
            packed[p, COMPONENTS * b + 3 : COMPONENTS * b + 4, :] = jnp.where(
                lane < counts[0, leaf], mass[:, here], 0.0
            )
        return carry

    lax.fori_loop(0, cols, pack, 0, unroll=cols <= 8)
    pl.semaphore_wait(barrier, cols + 1)

    def across(o):
        peer = lax.rem(c + o, cols)
        return pltpu.make_async_remote_copy(
            src_ref=packed.at[peer], dst_ref=table.at[0, c],
            send_sem=send.at[peer], recv_sem=recv.at[c],
            device_id=(r, peer), device_id_type=MESH,
        )

    def along(src, p, to_up):
        return pltpu.make_async_remote_copy(
            src_ref=src, dst_ref=table.at[1 if to_up else 2, p],
            send_sem=(up_send if to_up else down_send).at[p],
            recv_sem=(low_recv if to_up else high_recv).at[p],
            device_id=(up if to_up else down, c), device_id_type=MESH,
        )

    def send_across(o, carry):
        across(o).start()
        return carry

    lax.fori_loop(1, cols, send_across, 0)
    along(packed.at[c], c, True).start()
    along(packed.at[c], c, False).start()
    own = pltpu.make_async_copy(packed.at[c], table.at[0, c], own_sem)
    own.start()

    def forward(o, carry):
        p = lax.bitwise_xor(c, o) if cols & (cols - 1) == 0 else lax.rem(c + o, cols)
        pltpu.make_async_remote_copy(
            src_ref=packed.at[p], dst_ref=table.at[0, p],
            send_sem=send.at[p], recv_sem=recv.at[p],
            device_id=(r, p), device_id_type=MESH,
        ).wait_recv()
        along(table.at[0, p], p, True).start()
        along(table.at[0, p], p, False).start()
        return carry

    lax.fori_loop(1, cols, forward, 0)
    own.wait()

    def settle_sends(o, carry):
        across(o).wait_send()
        return carry

    lax.fori_loop(1, cols, settle_sends, 0)

    def settle(p, carry):
        for to_up in (True, False):
            copy = along(table.at[0, p], p, to_up)
            copy.wait_send()
            copy.wait_recv()
        return carry

    lax.fori_loop(0, cols, settle, 0)


def exchange(rows, cols, positions, masses, counts):
    leaves = counts.shape[1]
    width = positions.shape[1] // leaves
    tile = COMPONENTS * (leaves // cols)
    dma = pltpu.SemaphoreType.DMA
    return pl.pallas_call(
        functools.partial(exchange_kernel, rows, cols),
        out_shape=jax.ShapeDtypeStruct((3, cols, tile, width), jnp.float32),
        in_specs=[pl.BlockSpec(memory_space=pltpu.HBM)] * 3,
        out_specs=pl.BlockSpec(memory_space=pltpu.VMEM),
        scratch_shapes=[
            pltpu.VMEM(positions.shape, jnp.float32),
            pltpu.VMEM(masses.shape, jnp.float32),
            pltpu.SMEM(counts.shape, jnp.int32),
            pltpu.VMEM((cols, tile, width), jnp.float32),
            dma((3,)), dma(()), dma((cols,)), dma((cols,)),
            dma((cols,)), dma((cols,)), dma((cols,)), dma((cols,)),
        ],
        compiler_params=pltpu.CompilerParams(collective_id=0, has_side_effects=True, vmem_limit_bytes=VMEM_LIMIT),
        name="exchange",
    )(positions, masses, counts)


def row_sums(parts, lane, sublane):
    shift = 8
    while len(parts) > 1:
        second = (lane & shift) != 0
        parts = [
            jnp.where(second, b, a) + pltpu.roll(jnp.where(second, a, b), shift, 1)
            for a, b in zip(parts[::2], parts[1::2])
        ]
        shift *= 2
    (total,) = parts
    width = total.shape[1]
    for shift in (1, 2, 4):
        second = (lane & shift) != 0
        total = total + jnp.where(
            second, pltpu.roll(total, shift, 1), pltpu.roll(total, width - shift, 1)
        )
    return jnp.sum(jnp.where((lane & 7) == sublane, total, 0.0), axis=0, keepdims=True)


def force_kernel(sources_hbm, table, out, sources, spread_targets, pulls, live, in_sem):
    width = table.shape[1]
    group = spread_targets.shape[0]
    per_list = sources.shape[0]
    lane = lax.broadcasted_iota(jnp.int32, (8, width), 1)
    sublane = lax.broadcasted_iota(jnp.int32, (8, width), 0)
    load = pltpu.make_async_copy(sources_hbm, sources, in_sem)
    load.start()

    def one_group(g, carry):
        def prepare(i, carry):
            row = pl.multiple_of((g * group + 2 * i) * COMPONENTS, 8)
            pair = table[pl.ds(row, 8), :]
            columns = pair.T
            for b in range(2):
                for axis in range(3):
                    at = COMPONENTS * b + axis
                    spread_targets[2 * i + b, axis] = jnp.broadcast_to(
                        columns[:, at : at + 1], (width, width)
                    )
                alive = pair[COMPONENTS * b + 3 : COMPONENTS * b + 4] > 0.0
                live[2 * i + b] = jnp.sum(alive.astype(jnp.int32))
            return carry

        lax.fori_loop(0, group // 2, prepare, 0, unroll=2)

        @pl.when(g == 0)
        def _():
            load.wait()

        def one_target(i, carry):
            ids = [sources[k, g * group + i] * COMPONENTS for k in range(per_list)]

            def one_chunk(n, carry):
                here = pl.ds(pl.multiple_of(n * CHUNK, CHUNK), CHUNK)
                tx, ty, tz = (spread_targets[i, axis, here, :] for axis in range(3))
                ax = ay = az = jnp.zeros((CHUNK, width), jnp.float32)
                for k in range(per_list):
                    dx = table[pl.ds(ids[k], 1), :] - tx
                    dy = table[pl.ds(ids[k] + 1, 1), :] - ty
                    dz = table[pl.ds(ids[k] + 2, 1), :] - tz
                    inverse = lax.rsqrt(softening + dx * dx + dy * dy + dz * dz)
                    weight = table[pl.ds(ids[k] + 3, 1), :] * inverse * (inverse * inverse)
                    ax, ay, az = ax + weight * dx, ay + weight * dy, az + weight * dz
                pulls[i, 0, here, :] = ax
                pulls[i, 1, here, :] = ay
                pulls[i, 2, here, :] = az
                return carry

            chunks = lax.div(live[i] + (CHUNK - 1), CHUNK)
            return lax.fori_loop(0, chunks, one_chunk, carry)

        lax.fori_loop(0, group, one_target, 0)

        def reduce(i, carry):
            t = g * group + i
            alive = table[pl.ds(t * COMPONENTS + 3, 1), :] > 0.0
            for axis in range(3):
                parts = [pulls[i, axis, 8 * n : 8 * n + 8, :] for n in range(width // 8)]
                out[axis : axis + 1, pl.ds(pl.multiple_of(t * width, width), width)] = jnp.where(
                    alive, row_sums(parts, lane, sublane), 0.0
                )
            return carry

        lax.fori_loop(0, group, reduce, 0, unroll=2)
        return carry

    lax.fori_loop(0, sources.shape[1] // group, one_group, 0)


def forces(table, sources):
    leaves, width = sources.shape[1], table.shape[1]
    group = GROUP if leaves % GROUP == 0 else leaves
    return pl.pallas_call(
        force_kernel,
        out_shape=jax.ShapeDtypeStruct((3, leaves * width), jnp.float32),
        in_specs=[pl.BlockSpec(memory_space=pltpu.HBM), pl.BlockSpec(memory_space=pltpu.VMEM)],
        out_specs=pl.BlockSpec(memory_space=pltpu.VMEM),
        scratch_shapes=[
            pltpu.SMEM(sources.shape, jnp.int32),
            pltpu.VMEM((group, 3, width, width), jnp.float32),
            pltpu.VMEM((group, 3, width, width), jnp.float32),
            pltpu.SMEM((group,), jnp.int32),
            pltpu.SemaphoreType.DMA(()),
        ],
        compiler_params=pltpu.CompilerParams(vmem_limit_bytes=VMEM_LIMIT),
        name="forces",
    )(sources, table)


def in_hbm(array):
    return pltpu.with_memory_space_constraint(array, pltpu.HBM)


def solution(mesh):
    rows, cols = mesh.shape["row"], mesh.shape["col"]

    def on_device(positions, masses, counts, sources):
        table = exchange(rows, cols, *(in_hbm(a) for a in (positions, masses, counts)))
        return forces(table.reshape(-1, table.shape[-1]), in_hbm(sources.T))

    return jax.shard_map(
        on_device,
        mesh=mesh,
        in_specs=(
            P(None, ("row", "col")),
            P(None, ("row", "col")),
            P(None, ("row", "col")),
            P(("row", "col"), None),
        ),
        out_specs=P(None, ("row", "col")),
        check_vma=False,
    )
```

```python
import functools

import jax
import jax.numpy as jnp
from jax import lax
from jax.experimental import pallas as pl
from jax.experimental.pallas import tpu as pltpu
from jax.sharding import PartitionSpec as P

softening = 2.5e-07
COMPONENTS = 4
CHUNK = 32
GROUP = 16
MESH = pl.DeviceIdType.MESH


def vmem_limit(leaves, width):
    return 8 * 2**20 + 12 * leaves * width * width


def exchange_kernel(
    rows, cols, pos_hbm, mass_hbm, counts_hbm, table, spread_targets,
    pos, mass, counts, packed, in_sems, own_sem, send, recv, up_send, down_send, low_recv, high_recv,
):
    r, c = lax.axis_index("row"), lax.axis_index("col")
    up, down = lax.rem(r + 1, rows), lax.rem(r + rows - 1, rows)
    loads = [
        pltpu.make_async_copy(src, dst, in_sems.at[i])
        for i, (src, dst) in enumerate(((pos_hbm, pos), (mass_hbm, mass), (counts_hbm, counts)))
    ]
    for load in loads:
        load.start()

    barrier = pltpu.get_barrier_semaphore()
    pl.semaphore_signal(barrier, inc=1, device_id=(up, c), device_id_type=MESH)
    pl.semaphore_signal(barrier, inc=1, device_id=(down, c), device_id_type=MESH)

    def greet(o, carry):
        peer = lax.rem(c + o, cols)
        pl.semaphore_signal(barrier, inc=1, device_id=(r, peer), device_id_type=MESH)
        return carry

    lax.fori_loop(1, cols, greet, 0)
    for load in loads:
        load.wait()

    tile = packed.shape[1]
    blk = tile // COMPONENTS
    width = packed.shape[2]
    lane = lax.broadcasted_iota(jnp.int32, (1, width), 1)

    def pack(p, carry):
        for b in range(blk):
            leaf = p * blk + b
            here = pl.ds(pl.multiple_of(leaf * width, width), width)
            packed[p, COMPONENTS * b : COMPONENTS * b + 3, :] = pos[:, here]
            packed[p, COMPONENTS * b + 3 : COMPONENTS * b + 4, :] = jnp.where(
                lane < counts[0, leaf], mass[:, here], 0.0
            )
        return carry

    lax.fori_loop(0, cols, pack, 0, unroll=cols <= 8)
    pl.semaphore_wait(barrier, cols + 1)

    def across(o):
        peer = lax.rem(c + o, cols)
        return pltpu.make_async_remote_copy(
            src_ref=packed.at[peer], dst_ref=table.at[0, c],
            send_sem=send.at[peer], recv_sem=recv.at[c],
            device_id=(r, peer), device_id_type=MESH,
        )

    def along(src, p, to_up):
        return pltpu.make_async_remote_copy(
            src_ref=src, dst_ref=table.at[1 if to_up else 2, p],
            send_sem=(up_send if to_up else down_send).at[p],
            recv_sem=(low_recv if to_up else high_recv).at[p],
            device_id=(up if to_up else down, c), device_id_type=MESH,
        )

    def send_across(o, carry):
        across(o).start()
        return carry

    lax.fori_loop(1, cols, send_across, 0)
    along(packed.at[c], c, True).start()
    along(packed.at[c], c, False).start()
    own = pltpu.make_async_copy(packed.at[c], table.at[0, c], own_sem)
    own.start()

    def forward(o, carry):
        p = lax.bitwise_xor(c, o) if cols & (cols - 1) == 0 else lax.rem(c + o, cols)
        pltpu.make_async_remote_copy(
            src_ref=packed.at[p], dst_ref=table.at[0, p],
            send_sem=send.at[p], recv_sem=recv.at[p],
            device_id=(r, p), device_id_type=MESH,
        ).wait_recv()
        along(table.at[0, p], p, True).start()
        along(table.at[0, p], p, False).start()
        return carry

    lax.fori_loop(1, cols, forward, 0)
    own.wait()

    def spread(p, carry):
        columns = table[0, p].T
        for b in range(blk):
            for axis in range(3):
                at = COMPONENTS * b + axis
                spread_targets[p * blk + b, axis] = jnp.broadcast_to(
                    columns[:, at : at + 1], (width, width)
                )
        return carry

    lax.fori_loop(0, cols, spread, 0, unroll=2)

    def settle_sends(o, carry):
        across(o).wait_send()
        return carry

    lax.fori_loop(1, cols, settle_sends, 0)

    def settle(p, carry):
        for to_up in (True, False):
            copy = along(table.at[0, p], p, to_up)
            copy.wait_send()
            copy.wait_recv()
        return carry

    lax.fori_loop(0, cols, settle, 0)


def exchange(rows, cols, positions, masses, counts):
    leaves = counts.shape[1]
    width = positions.shape[1] // leaves
    tile = COMPONENTS * (leaves // cols)
    dma = pltpu.SemaphoreType.DMA
    return pl.pallas_call(
        functools.partial(exchange_kernel, rows, cols),
        out_shape=(
            jax.ShapeDtypeStruct((3, cols, tile, width), jnp.float32),
            jax.ShapeDtypeStruct((leaves, 3, width, width), jnp.float32),
        ),
        in_specs=[pl.BlockSpec(memory_space=pltpu.HBM)] * 3,
        out_specs=(pl.BlockSpec(memory_space=pltpu.VMEM),) * 2,
        scratch_shapes=[
            pltpu.VMEM(positions.shape, jnp.float32),
            pltpu.VMEM(masses.shape, jnp.float32),
            pltpu.SMEM(counts.shape, jnp.int32),
            pltpu.VMEM((cols, tile, width), jnp.float32),
            dma((3,)), dma(()), dma((cols,)), dma((cols,)),
            dma((cols,)), dma((cols,)), dma((cols,)), dma((cols,)),
        ],
        compiler_params=pltpu.CompilerParams(collective_id=0, has_side_effects=True, vmem_limit_bytes=vmem_limit(leaves, width)),
        name="exchange",
    )(positions, masses, counts)


def row_sums(parts, lane, sublane):
    shift = 8
    while len(parts) > 1:
        second = (lane & shift) != 0
        parts = [
            jnp.where(second, b, a) + pltpu.roll(jnp.where(second, a, b), shift, 1)
            for a, b in zip(parts[::2], parts[1::2])
        ]
        shift *= 2
    (total,) = parts
    width = total.shape[1]
    for shift in (1, 2, 4):
        second = (lane & shift) != 0
        total = total + jnp.where(
            second, pltpu.roll(total, shift, 1), pltpu.roll(total, width - shift, 1)
        )
    return jnp.sum(jnp.where((lane & 7) == sublane, total, 0.0), axis=0, keepdims=True)


def force_kernel(sources_hbm, table, spread_targets, out, sources, pulls, live, in_sem):
    width = table.shape[1]
    group = pulls.shape[0]
    per_list = sources.shape[0]
    lane = lax.broadcasted_iota(jnp.int32, (8, width), 1)
    sublane = lax.broadcasted_iota(jnp.int32, (8, width), 0)
    load = pltpu.make_async_copy(sources_hbm, sources, in_sem)
    load.start()

    def one_group(g, carry):
        def count(i, carry):
            alive = table[pl.ds((g * group + i) * COMPONENTS + 3, 1), :] > 0.0
            live[i] = jnp.sum(alive.astype(jnp.int32))
            return carry

        lax.fori_loop(0, group, count, 0, unroll=True)

        @pl.when(g == 0)
        def _():
            load.wait()

        def one_target(i, carry):
            ids = [sources[k, g * group + i] * COMPONENTS for k in range(per_list)]

            def one_chunk(n, carry):
                here = pl.ds(pl.multiple_of(n * CHUNK, CHUNK), CHUNK)
                tx, ty, tz = (spread_targets[g * group + i, axis, here, :] for axis in range(3))
                ax = ay = az = jnp.zeros((CHUNK, width), jnp.float32)
                for k in range(per_list):
                    dx = table[pl.ds(ids[k], 1), :] - tx
                    dy = table[pl.ds(ids[k] + 1, 1), :] - ty
                    dz = table[pl.ds(ids[k] + 2, 1), :] - tz
                    inverse = lax.rsqrt(softening + dx * dx + dy * dy + dz * dz)
                    weight = table[pl.ds(ids[k] + 3, 1), :] * inverse * (inverse * inverse)
                    ax, ay, az = ax + weight * dx, ay + weight * dy, az + weight * dz
                pulls[i, 0, here, :] = ax
                pulls[i, 1, here, :] = ay
                pulls[i, 2, here, :] = az
                return carry

            chunks = lax.div(live[i] + (CHUNK - 1), CHUNK)
            return lax.fori_loop(0, chunks, one_chunk, carry)

        lax.fori_loop(0, group, one_target, 0)

        def reduce(i, carry):
            t = g * group + i
            alive = table[pl.ds(t * COMPONENTS + 3, 1), :] > 0.0
            for axis in range(3):
                parts = [pulls[i, axis, 8 * n : 8 * n + 8, :] for n in range(width // 8)]
                out[axis : axis + 1, pl.ds(pl.multiple_of(t * width, width), width)] = jnp.where(
                    alive, row_sums(parts, lane, sublane), 0.0
                )
            return carry

        lax.fori_loop(0, group, reduce, 0, unroll=8)
        return carry

    lax.fori_loop(0, sources.shape[1] // group, one_group, 0)


def forces(table, spread_targets, sources):
    leaves, width = sources.shape[1], table.shape[1]
    group = GROUP if leaves % GROUP == 0 else leaves
    return pl.pallas_call(
        force_kernel,
        out_shape=jax.ShapeDtypeStruct((3, leaves * width), jnp.float32),
        in_specs=[pl.BlockSpec(memory_space=pltpu.HBM)] + [pl.BlockSpec(memory_space=pltpu.VMEM)] * 2,
        out_specs=pl.BlockSpec(memory_space=pltpu.VMEM),
        scratch_shapes=[
            pltpu.SMEM(sources.shape, jnp.int32),
            pltpu.VMEM((group, 3, width, width), jnp.float32),
            pltpu.SMEM((group,), jnp.int32),
            pltpu.SemaphoreType.DMA(()),
        ],
        compiler_params=pltpu.CompilerParams(vmem_limit_bytes=vmem_limit(leaves, width)),
        name="forces",
    )(sources, table, spread_targets)


def in_hbm(array):
    return pltpu.with_memory_space_constraint(array, pltpu.HBM)


def solution(mesh):
    rows, cols = mesh.shape["row"], mesh.shape["col"]

    def on_device(positions, masses, counts, sources):
        table, spread_targets = exchange(rows, cols, *(in_hbm(a) for a in (positions, masses, counts)))
        return forces(table.reshape(-1, table.shape[-1]), spread_targets, in_hbm(sources.T))

    return jax.shard_map(
        on_device,
        mesh=mesh,
        in_specs=(
            P(None, ("row", "col")),
            P(None, ("row", "col")),
            P(None, ("row", "col")),
            P(("row", "col"), None),
        ),
        out_specs=P(None, ("row", "col")),
        check_vma=False,
    )
```

```python
import functools

import jax
import jax.numpy as jnp
from jax import lax
from jax.experimental import pallas as pl
from jax.experimental.pallas import tpu as pltpu
from jax.sharding import PartitionSpec as P

softening = 2.5e-07
COMPONENTS = 4
CHUNK = 32
GROUP = 16
MESH = pl.DeviceIdType.MESH


def vmem_limit(leaves, width):
    return 8 * 2**20 + 12 * leaves * width * width


def exchange_kernel(
    rows, cols, pos_hbm, mass_hbm, counts_hbm, table, spread_targets,
    pos, mass, counts, packed, in_sems, own_sem, send, recv, up_send, down_send, low_recv, high_recv,
):
    r, c = lax.axis_index("row"), lax.axis_index("col")
    up, down = lax.rem(r + 1, rows), lax.rem(r + rows - 1, rows)
    loads = [
        pltpu.make_async_copy(src, dst, in_sems.at[i])
        for i, (src, dst) in enumerate(((pos_hbm, pos), (mass_hbm, mass), (counts_hbm, counts)))
    ]
    for load in loads:
        load.start()

    barrier = pltpu.get_barrier_semaphore()
    pl.semaphore_signal(barrier, inc=1, device_id=(up, c), device_id_type=MESH)
    pl.semaphore_signal(barrier, inc=1, device_id=(down, c), device_id_type=MESH)

    def greet(o, carry):
        peer = lax.rem(c + o, cols)
        pl.semaphore_signal(barrier, inc=1, device_id=(r, peer), device_id_type=MESH)
        return carry

    lax.fori_loop(1, cols, greet, 0)
    for load in loads:
        load.wait()

    tile = packed.shape[1]
    blk = tile // COMPONENTS
    width = packed.shape[2]
    lane = lax.broadcasted_iota(jnp.int32, (1, width), 1)

    def pack(p, carry):
        for b in range(blk):
            leaf = p * blk + b
            here = pl.ds(pl.multiple_of(leaf * width, width), width)
            packed[p, COMPONENTS * b : COMPONENTS * b + 3, :] = pos[:, here]
            packed[p, COMPONENTS * b + 3 : COMPONENTS * b + 4, :] = jnp.where(
                lane < counts[0, leaf], mass[:, here], 0.0
            )
        return carry

    lax.fori_loop(0, cols, pack, 0, unroll=cols <= 8)
    pl.semaphore_wait(barrier, cols + 1)

    def across(o):
        peer = lax.rem(c + o, cols)
        return pltpu.make_async_remote_copy(
            src_ref=packed.at[peer], dst_ref=table.at[0, c],
            send_sem=send.at[peer], recv_sem=recv.at[c],
            device_id=(r, peer), device_id_type=MESH,
        )

    def along(src, p, to_up):
        return pltpu.make_async_remote_copy(
            src_ref=src, dst_ref=table.at[1 if to_up else 2, p],
            send_sem=(up_send if to_up else down_send).at[p],
            recv_sem=(low_recv if to_up else high_recv).at[p],
            device_id=(up if to_up else down, c), device_id_type=MESH,
        )

    def send_across(o, carry):
        across(o).start()
        return carry

    lax.fori_loop(1, cols, send_across, 0)
    along(packed.at[c], c, True).start()
    along(packed.at[c], c, False).start()
    own = pltpu.make_async_copy(packed.at[c], table.at[0, c], own_sem)
    own.start()

    def forward(o, carry):
        p = lax.bitwise_xor(c, o) if cols & (cols - 1) == 0 else lax.rem(c + o, cols)
        pltpu.make_async_remote_copy(
            src_ref=packed.at[p], dst_ref=table.at[0, p],
            send_sem=send.at[p], recv_sem=recv.at[p],
            device_id=(r, p), device_id_type=MESH,
        ).wait_recv()
        along(table.at[0, p], p, True).start()
        along(table.at[0, p], p, False).start()
        return carry

    lax.fori_loop(1, cols, forward, 0)
    own.wait()

    def spread(p, carry):
        columns = table[0, p].T
        for b in range(blk):
            for axis in range(3):
                at = COMPONENTS * b + axis
                spread_targets[p * blk + b, axis] = jnp.broadcast_to(
                    columns[:, at : at + 1], (width, width)
                )
        return carry

    lax.fori_loop(0, cols, spread, 0, unroll=2)

    def settle_sends(o, carry):
        across(o).wait_send()
        return carry

    lax.fori_loop(1, cols, settle_sends, 0)

    def settle(p, carry):
        for to_up in (True, False):
            copy = along(table.at[0, p], p, to_up)
            copy.wait_send()
            copy.wait_recv()
        return carry

    lax.fori_loop(0, cols, settle, 0)


def exchange(rows, cols, positions, masses, counts):
    leaves = counts.shape[1]
    width = positions.shape[1] // leaves
    tile = COMPONENTS * (leaves // cols)
    dma = pltpu.SemaphoreType.DMA
    return pl.pallas_call(
        functools.partial(exchange_kernel, rows, cols),
        out_shape=(
            jax.ShapeDtypeStruct((3, cols, tile, width), jnp.float32),
            jax.ShapeDtypeStruct((leaves, 3, width, width), jnp.float32),
        ),
        in_specs=[pl.BlockSpec(memory_space=pltpu.HBM)] * 3,
        out_specs=(pl.BlockSpec(memory_space=pltpu.VMEM),) * 2,
        scratch_shapes=[
            pltpu.VMEM(positions.shape, jnp.float32),
            pltpu.VMEM(masses.shape, jnp.float32),
            pltpu.SMEM(counts.shape, jnp.int32),
            pltpu.VMEM((cols, tile, width), jnp.float32),
            dma((3,)), dma(()), dma((cols,)), dma((cols,)),
            dma((cols,)), dma((cols,)), dma((cols,)), dma((cols,)),
        ],
        compiler_params=pltpu.CompilerParams(collective_id=0, has_side_effects=True, vmem_limit_bytes=vmem_limit(leaves, width)),
        name="exchange",
    )(positions, masses, counts)


def merge(parts, shift, lane):
    second = (lane & shift) != 0
    return [
        jnp.where(second, b, a) + pltpu.roll(jnp.where(second, a, b), shift, 1)
        for a, b in zip(parts[::2], parts[1::2])
    ]


def merge_chunk(pull, lane):
    parts = [pull[8 * n : 8 * n + 8] for n in range(CHUNK // 8)]
    shift = 8
    while len(parts) > 1:
        parts = merge(parts, shift, lane)
        shift *= 2
    return parts[0]


def row_sums(parts, lane, sublane):
    shift = CHUNK
    while len(parts) > 1:
        parts = merge(parts, shift, lane)
        shift *= 2
    (total,) = parts
    width = total.shape[1]
    for shift in (1, 2, 4):
        second = (lane & shift) != 0
        total = total + jnp.where(
            second, pltpu.roll(total, shift, 1), pltpu.roll(total, width - shift, 1)
        )
    return jnp.sum(jnp.where((lane & 7) == sublane, total, 0.0), axis=0, keepdims=True)


def force_kernel(sources_hbm, table, spread_targets, out, sources, pull, merged, live, in_sem):
    width = table.shape[1]
    group = live.shape[0]
    per_leaf = width // CHUNK
    per_list = sources.shape[0]
    lane = lax.broadcasted_iota(jnp.int32, (8, width), 1)
    sublane = lax.broadcasted_iota(jnp.int32, (8, width), 0)
    load = pltpu.make_async_copy(sources_hbm, sources, in_sem)
    load.start()

    def one_group(g, carry):
        def count(i, carry):
            alive = table[pl.ds((g * group + i) * COMPONENTS + 3, 1), :] > 0.0
            live[i] = jnp.sum(alive.astype(jnp.int32))
            return carry

        lax.fori_loop(0, group, count, 0, unroll=True)

        @pl.when(g == 0)
        def _():
            load.wait()

        def one_target(i, carry):
            ids = [sources[k, g * group + i] * COMPONENTS for k in range(per_list)]

            def one_chunk(n, before):
                for axis in range(3):
                    merged[before, axis] = merge_chunk(pull[axis], lane)
                here = pl.ds(pl.multiple_of(n * CHUNK, CHUNK), CHUNK)
                tx, ty, tz = (spread_targets[g * group + i, axis, here, :] for axis in range(3))
                ax = ay = az = jnp.zeros((CHUNK, width), jnp.float32)
                for k in range(per_list):
                    dx = table[pl.ds(ids[k], 1), :] - tx
                    dy = table[pl.ds(ids[k] + 1, 1), :] - ty
                    dz = table[pl.ds(ids[k] + 2, 1), :] - tz
                    inverse = lax.rsqrt(softening + dx * dx + dy * dy + dz * dz)
                    weight = table[pl.ds(ids[k] + 3, 1), :] * inverse * (inverse * inverse)
                    ax, ay, az = ax + weight * dx, ay + weight * dy, az + weight * dz
                pull[0], pull[1], pull[2] = ax, ay, az
                return i * per_leaf + n

            chunks = lax.div(live[i] + (CHUNK - 1), CHUNK)
            return lax.fori_loop(0, chunks, one_chunk, carry)

        last = lax.fori_loop(0, group, one_target, group * per_leaf)
        for axis in range(3):
            merged[last, axis] = merge_chunk(pull[axis], lane)

        def reduce(i, carry):
            t = g * group + i
            alive = table[pl.ds(t * COMPONENTS + 3, 1), :] > 0.0
            for axis in range(3):
                parts = [merged[i * per_leaf + n, axis] for n in range(per_leaf)]
                out[axis : axis + 1, pl.ds(pl.multiple_of(t * width, width), width)] = jnp.where(
                    alive, row_sums(parts, lane, sublane), 0.0
                )
            return carry

        lax.fori_loop(0, group, reduce, 0, unroll=8)
        return carry

    lax.fori_loop(0, sources.shape[1] // group, one_group, 0)


def forces(table, spread_targets, sources):
    leaves, width = sources.shape[1], table.shape[1]
    group = GROUP if leaves % GROUP == 0 else leaves
    return pl.pallas_call(
        force_kernel,
        out_shape=jax.ShapeDtypeStruct((3, leaves * width), jnp.float32),
        in_specs=[pl.BlockSpec(memory_space=pltpu.HBM)] + [pl.BlockSpec(memory_space=pltpu.VMEM)] * 2,
        out_specs=pl.BlockSpec(memory_space=pltpu.VMEM),
        scratch_shapes=[
            pltpu.SMEM(sources.shape, jnp.int32),
            pltpu.VMEM((3, CHUNK, width), jnp.float32),
            pltpu.VMEM((group * (width // CHUNK) + 1, 3, 8, width), jnp.float32),
            pltpu.SMEM((group,), jnp.int32),
            pltpu.SemaphoreType.DMA(()),
        ],
        compiler_params=pltpu.CompilerParams(vmem_limit_bytes=vmem_limit(leaves, width)),
        name="forces",
    )(sources, table, spread_targets)


def in_hbm(array):
    return pltpu.with_memory_space_constraint(array, pltpu.HBM)


def solution(mesh):
    rows, cols = mesh.shape["row"], mesh.shape["col"]

    def on_device(positions, masses, counts, sources):
        table, spread_targets = exchange(rows, cols, *(in_hbm(a) for a in (positions, masses, counts)))
        return forces(table.reshape(-1, table.shape[-1]), spread_targets, in_hbm(sources.T))

    return jax.shard_map(
        on_device,
        mesh=mesh,
        in_specs=(
            P(None, ("row", "col")),
            P(None, ("row", "col")),
            P(None, ("row", "col")),
            P(("row", "col"), None),
        ),
        out_specs=P(None, ("row", "col")),
        check_vma=False,
    )
```

```python
import functools

import jax
import jax.numpy as jnp
from jax import lax
from jax.experimental import pallas as pl
from jax.experimental.pallas import tpu as pltpu
from jax.sharding import PartitionSpec as P

softening = 2.5e-07
COMPONENTS = 4
CHUNK = 32
GROUP = 16
MESH = pl.DeviceIdType.MESH


def vmem_limit(leaves, width):
    return 8 * 2**20 + 12 * leaves * width * width


def exchange_kernel(
    rows, cols, pos_hbm, mass_hbm, counts_hbm, table, spread_targets,
    pos, mass, counts, packed, in_sems, own_sem, send, recv, up_send, down_send, low_recv, high_recv,
):
    r, c = lax.axis_index("row"), lax.axis_index("col")
    up, down = lax.rem(r + 1, rows), lax.rem(r + rows - 1, rows)
    loads = [
        pltpu.make_async_copy(src, dst, in_sems.at[i])
        for i, (src, dst) in enumerate(((pos_hbm, pos), (mass_hbm, mass), (counts_hbm, counts)))
    ]
    for load in loads:
        load.start()

    barrier = pltpu.get_barrier_semaphore()
    pl.semaphore_signal(barrier, inc=1, device_id=(up, c), device_id_type=MESH)
    pl.semaphore_signal(barrier, inc=1, device_id=(down, c), device_id_type=MESH)

    def greet(o, carry):
        peer = lax.rem(c + o, cols)
        pl.semaphore_signal(barrier, inc=1, device_id=(r, peer), device_id_type=MESH)
        return carry

    lax.fori_loop(1, cols, greet, 0)
    for load in loads:
        load.wait()

    tile = packed.shape[1]
    blk = tile // COMPONENTS
    width = packed.shape[2]
    lane = lax.broadcasted_iota(jnp.int32, (1, width), 1)

    def pack(p, carry):
        for b in range(blk):
            leaf = p * blk + b
            here = pl.ds(pl.multiple_of(leaf * width, width), width)
            packed[p, COMPONENTS * b : COMPONENTS * b + 3, :] = pos[:, here]
            packed[p, COMPONENTS * b + 3 : COMPONENTS * b + 4, :] = jnp.where(
                lane < counts[0, leaf], mass[:, here], 0.0
            )
        return carry

    lax.fori_loop(0, cols, pack, 0, unroll=cols <= 8)
    pl.semaphore_wait(barrier, cols + 1)

    def across(o):
        peer = lax.rem(c + o, cols)
        return pltpu.make_async_remote_copy(
            src_ref=packed.at[peer], dst_ref=table.at[0, c],
            send_sem=send.at[peer], recv_sem=recv.at[c],
            device_id=(r, peer), device_id_type=MESH,
        )

    def along(src, p, to_up):
        return pltpu.make_async_remote_copy(
            src_ref=src, dst_ref=table.at[1 if to_up else 2, p],
            send_sem=(up_send if to_up else down_send).at[p],
            recv_sem=(low_recv if to_up else high_recv).at[p],
            device_id=(up if to_up else down, c), device_id_type=MESH,
        )

    def send_across(o, carry):
        across(o).start()
        return carry

    lax.fori_loop(1, cols, send_across, 0)
    along(packed.at[c], c, True).start()
    along(packed.at[c], c, False).start()
    own = pltpu.make_async_copy(packed.at[c], table.at[0, c], own_sem)
    own.start()

    def forward(o, carry):
        p = lax.bitwise_xor(c, o) if cols & (cols - 1) == 0 else lax.rem(c + o, cols)
        pltpu.make_async_remote_copy(
            src_ref=packed.at[p], dst_ref=table.at[0, p],
            send_sem=send.at[p], recv_sem=recv.at[p],
            device_id=(r, p), device_id_type=MESH,
        ).wait_recv()
        along(table.at[0, p], p, True).start()
        along(table.at[0, p], p, False).start()
        return carry

    lax.fori_loop(1, cols, forward, 0)
    own.wait()

    def spread(p, carry):
        columns = table[0, p].T
        for b in range(blk):
            for axis in range(3):
                at = COMPONENTS * b + axis
                spread_targets[p * blk + b, axis] = jnp.broadcast_to(
                    columns[:, at : at + 1], (width, width)
                )
        return carry

    lax.fori_loop(0, cols, spread, 0, unroll=2)

    def settle_sends(o, carry):
        across(o).wait_send()
        return carry

    lax.fori_loop(1, cols, settle_sends, 0)

    def settle(p, carry):
        for to_up in (True, False):
            copy = along(table.at[0, p], p, to_up)
            copy.wait_send()
            copy.wait_recv()
        return carry

    lax.fori_loop(0, cols, settle, 0)


def exchange(rows, cols, positions, masses, counts):
    leaves = counts.shape[1]
    width = positions.shape[1] // leaves
    tile = COMPONENTS * (leaves // cols)
    dma = pltpu.SemaphoreType.DMA
    return pl.pallas_call(
        functools.partial(exchange_kernel, rows, cols),
        out_shape=(
            jax.ShapeDtypeStruct((3, cols, tile, width), jnp.float32),
            jax.ShapeDtypeStruct((leaves, 3, width, width), jnp.float32),
        ),
        in_specs=[pl.BlockSpec(memory_space=pltpu.HBM)] * 3,
        out_specs=(pl.BlockSpec(memory_space=pltpu.VMEM),) * 2,
        scratch_shapes=[
            pltpu.VMEM(positions.shape, jnp.float32),
            pltpu.VMEM(masses.shape, jnp.float32),
            pltpu.SMEM(counts.shape, jnp.int32),
            pltpu.VMEM((cols, tile, width), jnp.float32),
            dma((3,)), dma(()), dma((cols,)), dma((cols,)),
            dma((cols,)), dma((cols,)), dma((cols,)), dma((cols,)),
        ],
        compiler_params=pltpu.CompilerParams(collective_id=0, has_side_effects=True, vmem_limit_bytes=vmem_limit(leaves, width)),
        name="exchange",
    )(positions, masses, counts)


def force_kernel(sources_hbm, table, spread_targets, out, sources, pulls, live, in_sem):
    width = table.shape[1]
    group = pulls.shape[0]
    per_list = sources.shape[0]
    load = pltpu.make_async_copy(sources_hbm, sources, in_sem)
    load.start()

    def one_group(g, carry):
        def count(i, carry):
            alive = table[pl.ds((g * group + i) * COMPONENTS + 3, 1), :] > 0.0
            live[i] = jnp.sum(alive.astype(jnp.int32))
            return carry

        lax.fori_loop(0, group, count, 0, unroll=True)

        @pl.when(g == 0)
        def _():
            load.wait()

        def one_target(i, carry):
            ids = [sources[k, g * group + i] * COMPONENTS for k in range(per_list)]

            def one_chunk(n, carry):
                here = pl.ds(pl.multiple_of(n * CHUNK, CHUNK), CHUNK)
                tx, ty, tz = (spread_targets[g * group + i, axis, here, :] for axis in range(3))
                ax = ay = az = jnp.zeros((CHUNK, width), jnp.float32)
                for k in range(per_list):
                    dx = table[pl.ds(ids[k], 1), :] - tx
                    dy = table[pl.ds(ids[k] + 1, 1), :] - ty
                    dz = table[pl.ds(ids[k] + 2, 1), :] - tz
                    inverse = lax.rsqrt(softening + dx * dx + dy * dy + dz * dz)
                    weight = table[pl.ds(ids[k] + 3, 1), :] * inverse * (inverse * inverse)
                    ax, ay, az = ax + weight * dx, ay + weight * dy, az + weight * dz
                pulls[i, 0, here, :] = ax
                pulls[i, 1, here, :] = ay
                pulls[i, 2, here, :] = az
                return carry

            chunks = lax.div(live[i] + (CHUNK - 1), CHUNK)
            return lax.fori_loop(0, chunks, one_chunk, carry)

        lax.fori_loop(0, group, one_target, 0)

        def reduce(i, carry):
            t = g * group + i
            alive = table[pl.ds(t * COMPONENTS + 3, 1), :] > 0.0
            for axis in range(3):
                total = jnp.sum(pulls[i, axis].T, axis=0, keepdims=True)
                out[axis : axis + 1, pl.ds(pl.multiple_of(t * width, width), width)] = jnp.where(
                    alive, total, 0.0
                )
            return carry

        lax.fori_loop(0, group, reduce, 0, unroll=8)
        return carry

    lax.fori_loop(0, sources.shape[1] // group, one_group, 0)


def forces(table, spread_targets, sources):
    leaves, width = sources.shape[1], table.shape[1]
    group = GROUP if leaves % GROUP == 0 else leaves
    return pl.pallas_call(
        force_kernel,
        out_shape=jax.ShapeDtypeStruct((3, leaves * width), jnp.float32),
        in_specs=[pl.BlockSpec(memory_space=pltpu.HBM)] + [pl.BlockSpec(memory_space=pltpu.VMEM)] * 2,
        out_specs=pl.BlockSpec(memory_space=pltpu.VMEM),
        scratch_shapes=[
            pltpu.SMEM(sources.shape, jnp.int32),
            pltpu.VMEM((group, 3, width, width), jnp.float32),
            pltpu.SMEM((group,), jnp.int32),
            pltpu.SemaphoreType.DMA(()),
        ],
        compiler_params=pltpu.CompilerParams(vmem_limit_bytes=vmem_limit(leaves, width)),
        name="forces",
    )(sources, table, spread_targets)


def in_hbm(array):
    return pltpu.with_memory_space_constraint(array, pltpu.HBM)


def solution(mesh):
    rows, cols = mesh.shape["row"], mesh.shape["col"]

    def on_device(positions, masses, counts, sources):
        table, spread_targets = exchange(rows, cols, *(in_hbm(a) for a in (positions, masses, counts)))
        return forces(table.reshape(-1, table.shape[-1]), spread_targets, in_hbm(sources.T))

    return jax.shard_map(
        on_device,
        mesh=mesh,
        in_specs=(
            P(None, ("row", "col")),
            P(None, ("row", "col")),
            P(None, ("row", "col")),
            P(("row", "col"), None),
        ),
        out_specs=P(None, ("row", "col")),
        check_vma=False,
    )
```

```python
import functools

import jax
import jax.numpy as jnp
from jax import lax
from jax.experimental import pallas as pl
from jax.experimental.pallas import tpu as pltpu
from jax.sharding import PartitionSpec as P

softening = 2.5e-07
COMPONENTS = 4
CHUNK = 32
GROUP = 16
MESH = pl.DeviceIdType.MESH


def vmem_limit(leaves, width):
    return 8 * 2**20 + 12 * leaves * width * width


def exchange_kernel(
    rows, cols, pos_hbm, mass_hbm, counts_hbm, sources_hbm, table, spread_targets, sources,
    pos, mass, counts, packed, in_sems, own_sem, send, recv, up_send, down_send, low_recv, high_recv,
):
    r, c = lax.axis_index("row"), lax.axis_index("col")
    up, down = lax.rem(r + 1, rows), lax.rem(r + rows - 1, rows)
    loads = [
        pltpu.make_async_copy(src, dst, in_sems.at[i])
        for i, (src, dst) in enumerate(((pos_hbm, pos), (mass_hbm, mass), (counts_hbm, counts), (sources_hbm, sources)))
    ]
    for load in loads:
        load.start()

    barrier = pltpu.get_barrier_semaphore()
    pl.semaphore_signal(barrier, inc=1, device_id=(up, c), device_id_type=MESH)
    pl.semaphore_signal(barrier, inc=1, device_id=(down, c), device_id_type=MESH)

    def greet(o, carry):
        peer = lax.rem(c + o, cols)
        pl.semaphore_signal(barrier, inc=1, device_id=(r, peer), device_id_type=MESH)
        return carry

    lax.fori_loop(1, cols, greet, 0)
    for load in loads[:3]:
        load.wait()

    tile = packed.shape[1]
    blk = tile // COMPONENTS
    width = packed.shape[2]
    lane = lax.broadcasted_iota(jnp.int32, (1, width), 1)

    def pack(p, carry):
        for b in range(blk):
            leaf = p * blk + b
            here = pl.ds(pl.multiple_of(leaf * width, width), width)
            packed[p, COMPONENTS * b : COMPONENTS * b + 3, :] = pos[:, here]
            packed[p, COMPONENTS * b + 3 : COMPONENTS * b + 4, :] = jnp.where(
                lane < counts[0, leaf], mass[:, here], 0.0
            )
        return carry

    lax.fori_loop(0, cols, pack, 0, unroll=cols <= 8)
    pl.semaphore_wait(barrier, cols + 1)

    def across(o):
        peer = lax.rem(c + o, cols)
        return pltpu.make_async_remote_copy(
            src_ref=packed.at[peer], dst_ref=table.at[0, c],
            send_sem=send.at[peer], recv_sem=recv.at[c],
            device_id=(r, peer), device_id_type=MESH,
        )

    def along(src, p, to_up):
        return pltpu.make_async_remote_copy(
            src_ref=src, dst_ref=table.at[1 if to_up else 2, p],
            send_sem=(up_send if to_up else down_send).at[p],
            recv_sem=(low_recv if to_up else high_recv).at[p],
            device_id=(up if to_up else down, c), device_id_type=MESH,
        )

    def send_across(o, carry):
        across(o).start()
        return carry

    lax.fori_loop(1, cols, send_across, 0)
    along(packed.at[c], c, True).start()
    along(packed.at[c], c, False).start()
    own = pltpu.make_async_copy(packed.at[c], table.at[0, c], own_sem)
    own.start()

    def forward(o, carry):
        p = lax.bitwise_xor(c, o) if cols & (cols - 1) == 0 else lax.rem(c + o, cols)
        pltpu.make_async_remote_copy(
            src_ref=packed.at[p], dst_ref=table.at[0, p],
            send_sem=send.at[p], recv_sem=recv.at[p],
            device_id=(r, p), device_id_type=MESH,
        ).wait_recv()
        along(table.at[0, p], p, True).start()
        along(table.at[0, p], p, False).start()
        return carry

    lax.fori_loop(1, cols, forward, 0)
    own.wait()

    def spread(p, carry):
        columns = table[0, p].T
        for b in range(blk):
            for axis in range(3):
                at = COMPONENTS * b + axis
                spread_targets[p * blk + b, axis] = jnp.broadcast_to(
                    columns[:, at : at + 1], (width, width)
                )
        return carry

    lax.fori_loop(0, cols, spread, 0, unroll=2)
    loads[3].wait()

    def settle_sends(o, carry):
        across(o).wait_send()
        return carry

    lax.fori_loop(1, cols, settle_sends, 0)

    def settle(p, carry):
        for to_up in (True, False):
            copy = along(table.at[0, p], p, to_up)
            copy.wait_send()
            copy.wait_recv()
        return carry

    lax.fori_loop(0, cols, settle, 0)


def exchange(rows, cols, positions, masses, counts, sources):
    leaves = counts.shape[1]
    width = positions.shape[1] // leaves
    tile = COMPONENTS * (leaves // cols)
    dma = pltpu.SemaphoreType.DMA
    return pl.pallas_call(
        functools.partial(exchange_kernel, rows, cols),
        out_shape=(
            jax.ShapeDtypeStruct((3, cols, tile, width), jnp.float32),
            jax.ShapeDtypeStruct((leaves, 3, width, width), jnp.float32),
            jax.ShapeDtypeStruct(sources.shape, jnp.int32),
        ),
        in_specs=[pl.BlockSpec(memory_space=pltpu.HBM)] * 4,
        out_specs=(pl.BlockSpec(memory_space=pltpu.VMEM),) * 3,
        scratch_shapes=[
            pltpu.VMEM(positions.shape, jnp.float32),
            pltpu.VMEM(masses.shape, jnp.float32),
            pltpu.SMEM(counts.shape, jnp.int32),
            pltpu.VMEM((cols, tile, width), jnp.float32),
            dma((4,)), dma(()), dma((cols,)), dma((cols,)),
            dma((cols,)), dma((cols,)), dma((cols,)), dma((cols,)),
        ],
        compiler_params=pltpu.CompilerParams(collective_id=0, has_side_effects=True, vmem_limit_bytes=vmem_limit(leaves, width)),
        name="exchange",
    )(positions, masses, counts, sources)


def force_kernel(sources_vmem, table, spread_targets, out, sources, pulls, live, in_sem):
    width = table.shape[1]
    group = pulls.shape[0]
    per_list = sources.shape[0]
    load = pltpu.make_async_copy(sources_vmem, sources, in_sem)
    load.start()

    def one_group(g, carry):
        def count(i, carry):
            alive = table[pl.ds((g * group + i) * COMPONENTS + 3, 1), :] > 0.0
            live[i] = jnp.sum(alive.astype(jnp.int32))
            return carry

        lax.fori_loop(0, group, count, 0, unroll=True)

        @pl.when(g == 0)
        def _():
            load.wait()

        def one_target(i, carry):
            ids = [sources[k, g * group + i] * COMPONENTS for k in range(per_list)]

            def one_chunk(n, carry):
                here = pl.ds(pl.multiple_of(n * CHUNK, CHUNK), CHUNK)
                tx, ty, tz = (spread_targets[g * group + i, axis, here, :] for axis in range(3))
                ax = ay = az = jnp.zeros((CHUNK, width), jnp.float32)
                for k in range(per_list):
                    dx = table[pl.ds(ids[k], 1), :] - tx
                    dy = table[pl.ds(ids[k] + 1, 1), :] - ty
                    dz = table[pl.ds(ids[k] + 2, 1), :] - tz
                    inverse = lax.rsqrt(softening + dx * dx + dy * dy + dz * dz)
                    weight = table[pl.ds(ids[k] + 3, 1), :] * inverse * (inverse * inverse)
                    ax, ay, az = ax + weight * dx, ay + weight * dy, az + weight * dz
                pulls[i, 0, here, :] = ax
                pulls[i, 1, here, :] = ay
                pulls[i, 2, here, :] = az
                return carry

            chunks = lax.div(live[i] + (CHUNK - 1), CHUNK)
            return lax.fori_loop(0, chunks, one_chunk, carry)

        lax.fori_loop(0, group, one_target, 0)

        def reduce(i, carry):
            t = g * group + i
            alive = table[pl.ds(t * COMPONENTS + 3, 1), :] > 0.0
            for axis in range(3):
                total = jnp.sum(pulls[i, axis].T, axis=0, keepdims=True)
                out[axis : axis + 1, pl.ds(pl.multiple_of(t * width, width), width)] = jnp.where(
                    alive, total, 0.0
                )
            return carry

        lax.fori_loop(0, group, reduce, 0, unroll=8)
        return carry

    lax.fori_loop(0, sources.shape[1] // group, one_group, 0)


def forces(table, spread_targets, sources):
    leaves, width = sources.shape[1], table.shape[1]
    group = GROUP if leaves % GROUP == 0 else leaves
    return pl.pallas_call(
        force_kernel,
        out_shape=jax.ShapeDtypeStruct((3, leaves * width), jnp.float32),
        in_specs=[pl.BlockSpec(memory_space=pltpu.VMEM)] * 3,
        out_specs=pl.BlockSpec(memory_space=pltpu.VMEM),
        scratch_shapes=[
            pltpu.SMEM(sources.shape, jnp.int32),
            pltpu.VMEM((group, 3, width, width), jnp.float32),
            pltpu.SMEM((group,), jnp.int32),
            pltpu.SemaphoreType.DMA(()),
        ],
        compiler_params=pltpu.CompilerParams(vmem_limit_bytes=vmem_limit(leaves, width)),
        name="forces",
    )(sources, table, spread_targets)


def in_hbm(array):
    return pltpu.with_memory_space_constraint(array, pltpu.HBM)


def solution(mesh):
    rows, cols = mesh.shape["row"], mesh.shape["col"]

    def on_device(positions, masses, counts, sources):
        args = (in_hbm(a) for a in (positions, masses, counts, sources.T))
        table, spread_targets, staged = exchange(rows, cols, *args)
        return forces(table.reshape(-1, table.shape[-1]), spread_targets, staged)

    return jax.shard_map(
        on_device,
        mesh=mesh,
        in_specs=(
            P(None, ("row", "col")),
            P(None, ("row", "col")),
            P(None, ("row", "col")),
            P(("row", "col"), None),
        ),
        out_specs=P(None, ("row", "col")),
        check_vma=False,
    )
```

```python
import functools

import jax
import jax.numpy as jnp
from jax import lax
from jax.experimental import pallas as pl
from jax.experimental.pallas import tpu as pltpu
from jax.sharding import PartitionSpec as P

softening = 2.5e-07
COMPONENTS = 4
CHUNK = 16
GROUP = 16
MESH = pl.DeviceIdType.MESH


def vmem_limit(leaves, width):
    return 8 * 2**20 + 12 * leaves * width * width


def exchange_kernel(
    rows, cols, pos_hbm, mass_hbm, counts_hbm, sources_hbm, table, spread_targets, sources,
    pos, mass, counts, packed, in_sems, own_sem, send, recv, up_send, down_send, low_recv, high_recv,
):
    r, c = lax.axis_index("row"), lax.axis_index("col")
    up, down = lax.rem(r + 1, rows), lax.rem(r + rows - 1, rows)
    loads = [
        pltpu.make_async_copy(src, dst, in_sems.at[i])
        for i, (src, dst) in enumerate(((pos_hbm, pos), (mass_hbm, mass), (counts_hbm, counts), (sources_hbm, sources)))
    ]
    for load in loads:
        load.start()

    barrier = pltpu.get_barrier_semaphore()
    pl.semaphore_signal(barrier, inc=1, device_id=(up, c), device_id_type=MESH)
    pl.semaphore_signal(barrier, inc=1, device_id=(down, c), device_id_type=MESH)

    def greet(o, carry):
        peer = lax.rem(c + o, cols)
        pl.semaphore_signal(barrier, inc=1, device_id=(r, peer), device_id_type=MESH)
        return carry

    lax.fori_loop(1, cols, greet, 0)
    for load in loads[:3]:
        load.wait()

    tile = packed.shape[1]
    blk = tile // COMPONENTS
    width = packed.shape[2]
    lane = lax.broadcasted_iota(jnp.int32, (1, width), 1)

    def pack(p, carry):
        for b in range(blk):
            leaf = p * blk + b
            here = pl.ds(pl.multiple_of(leaf * width, width), width)
            packed[p, COMPONENTS * b : COMPONENTS * b + 3, :] = pos[:, here]
            packed[p, COMPONENTS * b + 3 : COMPONENTS * b + 4, :] = jnp.where(
                lane < counts[0, leaf], mass[:, here], 0.0
            )
        return carry

    lax.fori_loop(0, cols, pack, 0, unroll=cols <= 8)
    pl.semaphore_wait(barrier, cols + 1)

    def across(o):
        peer = lax.rem(c + o, cols)
        return pltpu.make_async_remote_copy(
            src_ref=packed.at[peer], dst_ref=table.at[0, c],
            send_sem=send.at[peer], recv_sem=recv.at[c],
            device_id=(r, peer), device_id_type=MESH,
        )

    def along(src, p, to_up):
        return pltpu.make_async_remote_copy(
            src_ref=src, dst_ref=table.at[1 if to_up else 2, p],
            send_sem=(up_send if to_up else down_send).at[p],
            recv_sem=(low_recv if to_up else high_recv).at[p],
            device_id=(up if to_up else down, c), device_id_type=MESH,
        )

    def send_across(o, carry):
        across(o).start()
        return carry

    lax.fori_loop(1, cols, send_across, 0)
    along(packed.at[c], c, True).start()
    along(packed.at[c], c, False).start()
    own = pltpu.make_async_copy(packed.at[c], table.at[0, c], own_sem)
    own.start()

    def forward(o, carry):
        p = lax.bitwise_xor(c, o) if cols & (cols - 1) == 0 else lax.rem(c + o, cols)
        pltpu.make_async_remote_copy(
            src_ref=packed.at[p], dst_ref=table.at[0, p],
            send_sem=send.at[p], recv_sem=recv.at[p],
            device_id=(r, p), device_id_type=MESH,
        ).wait_recv()
        along(table.at[0, p], p, True).start()
        along(table.at[0, p], p, False).start()
        return carry

    lax.fori_loop(1, cols, forward, 0)
    own.wait()

    def spread(p, carry):
        columns = table[0, p].T
        for b in range(blk):
            for axis in range(3):
                at = COMPONENTS * b + axis
                spread_targets[p * blk + b, axis] = jnp.broadcast_to(
                    columns[:, at : at + 1], (width, width)
                )
        return carry

    lax.fori_loop(0, cols, spread, 0, unroll=2)
    loads[3].wait()

    def settle_sends(o, carry):
        across(o).wait_send()
        return carry

    lax.fori_loop(1, cols, settle_sends, 0)

    def settle(p, carry):
        for to_up in (True, False):
            copy = along(table.at[0, p], p, to_up)
            copy.wait_send()
            copy.wait_recv()
        return carry

    lax.fori_loop(0, cols, settle, 0)


def exchange(rows, cols, positions, masses, counts, sources):
    leaves = counts.shape[1]
    width = positions.shape[1] // leaves
    tile = COMPONENTS * (leaves // cols)
    dma = pltpu.SemaphoreType.DMA
    return pl.pallas_call(
        functools.partial(exchange_kernel, rows, cols),
        out_shape=(
            jax.ShapeDtypeStruct((3, cols, tile, width), jnp.float32),
            jax.ShapeDtypeStruct((leaves, 3, width, width), jnp.float32),
            jax.ShapeDtypeStruct(sources.shape, jnp.int32),
        ),
        in_specs=[pl.BlockSpec(memory_space=pltpu.HBM)] * 4,
        out_specs=(pl.BlockSpec(memory_space=pltpu.VMEM),) * 3,
        scratch_shapes=[
            pltpu.VMEM(positions.shape, jnp.float32),
            pltpu.VMEM(masses.shape, jnp.float32),
            pltpu.SMEM(counts.shape, jnp.int32),
            pltpu.VMEM((cols, tile, width), jnp.float32),
            dma((4,)), dma(()), dma((cols,)), dma((cols,)),
            dma((cols,)), dma((cols,)), dma((cols,)), dma((cols,)),
        ],
        compiler_params=pltpu.CompilerParams(collective_id=0, has_side_effects=True, vmem_limit_bytes=vmem_limit(leaves, width)),
        name="exchange",
    )(positions, masses, counts, sources)


def force_kernel(sources_vmem, table, spread_targets, out, sources, pulls, live, in_sem):
    width = table.shape[1]
    group = pulls.shape[0]
    per_list = sources.shape[0]
    load = pltpu.make_async_copy(sources_vmem, sources, in_sem)
    load.start()

    def one_group(g, carry):
        def count(i, carry):
            alive = table[pl.ds((g * group + i) * COMPONENTS + 3, 1), :] > 0.0
            live[i] = jnp.sum(alive.astype(jnp.int32))
            return carry

        lax.fori_loop(0, group, count, 0, unroll=True)

        @pl.when(g == 0)
        def _():
            load.wait()

        def one_target(i, carry):
            ids = [sources[k, g * group + i] * COMPONENTS for k in range(per_list)]

            def one_chunk(n, carry):
                here = pl.ds(pl.multiple_of(n * CHUNK, CHUNK), CHUNK)
                tx, ty, tz = (spread_targets[g * group + i, axis, here, :] for axis in range(3))
                ax = ay = az = jnp.zeros((CHUNK, width), jnp.float32)
                for k in range(per_list):
                    dx = table[pl.ds(ids[k], 1), :] - tx
                    dy = table[pl.ds(ids[k] + 1, 1), :] - ty
                    dz = table[pl.ds(ids[k] + 2, 1), :] - tz
                    inverse = lax.rsqrt(softening + dx * dx + dy * dy + dz * dz)
                    weight = table[pl.ds(ids[k] + 3, 1), :] * inverse * (inverse * inverse)
                    ax, ay, az = ax + weight * dx, ay + weight * dy, az + weight * dz
                pulls[i, 0, here, :] = ax
                pulls[i, 1, here, :] = ay
                pulls[i, 2, here, :] = az
                return carry

            chunks = lax.div(live[i] + (CHUNK - 1), CHUNK)
            return lax.fori_loop(0, chunks, one_chunk, carry)

        lax.fori_loop(0, group, one_target, 0)

        def reduce(i, carry):
            t = g * group + i
            alive = table[pl.ds(t * COMPONENTS + 3, 1), :] > 0.0
            for axis in range(3):
                total = jnp.sum(pulls[i, axis].T, axis=0, keepdims=True)
                out[axis : axis + 1, pl.ds(pl.multiple_of(t * width, width), width)] = jnp.where(
                    alive, total, 0.0
                )
            return carry

        lax.fori_loop(0, group, reduce, 0, unroll=8)
        return carry

    lax.fori_loop(0, sources.shape[1] // group, one_group, 0)


def forces(table, spread_targets, sources):
    leaves, width = sources.shape[1], table.shape[1]
    group = GROUP if leaves % GROUP == 0 else leaves
    return pl.pallas_call(
        force_kernel,
        out_shape=jax.ShapeDtypeStruct((3, leaves * width), jnp.float32),
        in_specs=[pl.BlockSpec(memory_space=pltpu.VMEM)] * 3,
        out_specs=pl.BlockSpec(memory_space=pltpu.VMEM),
        scratch_shapes=[
            pltpu.SMEM(sources.shape, jnp.int32),
            pltpu.VMEM((group, 3, width, width), jnp.float32),
            pltpu.SMEM((group,), jnp.int32),
            pltpu.SemaphoreType.DMA(()),
        ],
        compiler_params=pltpu.CompilerParams(vmem_limit_bytes=vmem_limit(leaves, width)),
        name="forces",
    )(sources, table, spread_targets)


def in_hbm(array):
    return pltpu.with_memory_space_constraint(array, pltpu.HBM)


def solution(mesh):
    rows, cols = mesh.shape["row"], mesh.shape["col"]

    def on_device(positions, masses, counts, sources):
        args = (in_hbm(a) for a in (positions, masses, counts, sources.T))
        table, spread_targets, staged = exchange(rows, cols, *args)
        return forces(table.reshape(-1, table.shape[-1]), spread_targets, staged)

    return jax.shard_map(
        on_device,
        mesh=mesh,
        in_specs=(
            P(None, ("row", "col")),
            P(None, ("row", "col")),
            P(None, ("row", "col")),
            P(("row", "col"), None),
        ),
        out_specs=P(None, ("row", "col")),
        check_vma=False,
    )
```
